32 devices in a mesh: parts: 2 (over y), tmpl: 4 (over z), sta: 4 (over x, core).
Axes of the slice: x: 2, y: 2, z: 4, core: 2. Of those that a mesh axis runs over, the one named last changes fastest.
Arguments:
- data: float32 [64, 3, 1280], P(('parts', 'sta'), None, 'tmpl'), parts along dimension 0, as said below
- templates: bfloat16 [32, 3, 16, 256], P('sta', None, 'tmpl'), as said below
- starts: int32 [32, 3, 16], P('sta', None, 'tmpl'), may hold values from 0 to 512
Outputs:
- network: float32 [32, 512], P(('parts', 'tmpl'), 'sta'), parts along dimension 0
The draws below stay inside these ranges and needn't reach their ends.
There are 2 independent parts, one for each index of `parts`. The reference program is written for one: setup_inputs(seed, part) draws one part's arguments, and reference() takes and returns one part's arrays. A program takes and returns all parts, laid end to end along the dimension named above; an argument that names none is the same for every part. Nothing has to cross between parts.
Inputs may be any that keep to these rules, and one draw needn't show every extreme that they name: `data`: finite samples. `templates`: finite samples.
All inputs are finite; a program needn't handle non-finite values.
Results may differ from the reference program's by a relative error of at most 0.0029.
Values sent between devices are 32-bit elements; how exact they have to be, the bound alone decides.
A program may use at most 64 MiB of HBM per device.

```python
import math
import jax
import jax.numpy as jnp
from jax import lax

TLEN = 256
MAXSHIFT = 512
LAGS = 512
TEMPLATES = 16
STATIONS = 32
SAMPLES = 1280


def draw_data(key, part):
    first_key, second_key = jax.random.split(key, 2)
    segments = (SAMPLES + 31) // 32
    levels = jax.random.uniform(second_key, (STATIONS, 3, segments), jnp.float32)
    random_part = jax.random.normal(first_key, (STATIONS, 3, SAMPLES), jnp.float32)
    envelope = jnp.exp(levels * math.log(10.0))
    envelope = jnp.repeat(envelope, 32, axis=2)[:, :, :SAMPLES]
    return (random_part * envelope).astype(jnp.float32)


def draw_templates(key, part):
    first_key, second_key, third_key = jax.random.split(key, 3)
    segments = (TLEN + 7) // 8
    random_part = jax.random.normal(first_key, (STATIONS, 3, TEMPLATES, TLEN), jnp.float32)
    row_scale = jnp.exp(jax.random.uniform(second_key, (STATIONS, 3, TEMPLATES, 1), jnp.float32) * math.log(10.0)) * 0.1
    levels = jax.random.uniform(third_key, (STATIONS, 3, TEMPLATES, segments), jnp.float32)
    envelope = jnp.repeat(jnp.exp(levels * math.log(3.0)), 8, axis=3)[:, :, :, :TLEN]
    return (random_part * row_scale * envelope).astype(jnp.bfloat16)


def with_ends(result, key, least, high):
    longest = result.shape.index(max(result.shape))
    spots = []
    for shift in (0, 1):
        where = [jax.random.randint(jax.random.fold_in(key, axis), (), 0, length) for axis, length in enumerate(result.shape)]
        where[longest] = (where[longest] + shift) % result.shape[longest]
        spots.append(tuple(where))
    return result.at[spots[0]].set(least).at[spots[1]].set(high)


def setup_inputs(seed: int = 0, part: int = 0) -> dict:
    streams_of = jax.random.split(jax.random.key(seed), 4)
    own_keys = jax.random.split(jax.random.fold_in(streams_of[3], part), 4)
    return {
        "data": draw_data(jax.random.fold_in(jax.random.fold_in(streams_of[3], part), 71), part),
        "templates": draw_templates(jax.random.fold_in(streams_of[3], 71), part),
        "starts": with_ends(jax.random.randint(streams_of[2], (STATIONS, 3, TEMPLATES), 0, MAXSHIFT + 1), jax.random.fold_in(streams_of[2], 1), 0, MAXSHIFT).astype(jnp.int32),
    }


EPS = 1e-06

def window_energy(trace):
    extent = LAGS + MAXSHIFT
    squares = trace * trace
    running = jnp.concatenate([jnp.zeros_like(squares[:, :1]), jnp.cumsum(squares, axis=1)], axis=1)
    return running[:, TLEN:TLEN + extent] - running[:, :extent]

def station_term(trace, waves, offsets):
    extent = LAGS + MAXSHIFT
    lowered = lax.optimization_barrier(trace.astype(jnp.bfloat16)).astype(jnp.float32)
    kernel = waves.astype(jnp.float32).reshape(-1, 1, waves.shape[-1])
    raw = lax.conv_general_dilated(lowered[None], kernel, (1,), 'VALID', dimension_numbers=('NCH', 'OIH', 'NCH'), feature_group_count=3, precision=lax.Precision.HIGHEST, preferred_element_type=jnp.float32)[0]
    raw = raw.reshape(3, waves.shape[1], -1)[:, :, :extent]
    energy = window_energy(trace)
    tnorm = lax.optimization_barrier(jnp.sum(waves.astype(jnp.float32) ** 2, axis=-1))
    index = offsets.astype(jnp.int32)[:, :, None] + jnp.arange(LAGS, dtype=jnp.int32)[None, None, :]
    aligned = jnp.take_along_axis(raw, index, axis=2)
    channel = jnp.arange(3, dtype=jnp.int32)[:, None, None]
    local = energy[channel, index]
    scale = TLEN * jnp.sqrt((tnorm[:, :, None] / TLEN + EPS) * (local / TLEN + EPS))
    return lax.optimization_barrier(jnp.sum(aligned / scale, axis=0))

def reference(data, templates, starts):

    def step(total, items):
        trace, waves, offsets = items
        return (total + station_term(trace, waves, offsets), None)
    start_total = jnp.zeros((templates.shape[2], LAGS), jnp.float32)
    total, _ = lax.scan(step, start_total, (data, templates, starts))
    return total
```

```python
import functools

import jax
import jax.numpy as jnp
from jax import lax
from jax.experimental import pallas as pl
from jax.experimental.pallas import tpu as pltpu
from jax.sharding import PartitionSpec as P

TLEN = 256
MAXSHIFT = 512
LAGS = 512
EXTENT = LAGS + MAXSHIFT
LANE = 128
CHUNKS = EXTENT // LANE
BAND = TLEN + LANE
ROWS = 16
EPS = 1e-06

MESH = pl.DeviceIdType.MESH


def kernel(
    peers, owners,
    starts_hbm, data_ref, templates_hbm, out_ref,
    starts_ref, templates_ref, local_sems, gathered, chunked, flat, bands, norms, inverse, lagged, partial_ref, arrived,
    data_send, data_recv, sum_send, sum_recv,
):
    channels, stations, width = data_ref.shape
    per_group = templates_ref.shape[2]
    groups = stations * channels
    samples = width * peers
    my_tmpl = lax.axis_index("tmpl")
    my_sta = lax.axis_index("sta")

    fetches = [
        pltpu.make_async_copy(templates_hbm, templates_ref, local_sems.at[0]),
        pltpu.make_async_copy(starts_hbm, starts_ref, local_sems.at[1]),
        pltpu.make_async_copy(data_ref, gathered.at[my_tmpl], local_sems.at[2]),
    ]
    for copy in fetches:
        copy.start()

    barrier = pltpu.get_barrier_semaphore()
    for step in range(1, peers):
        pl.semaphore_signal(
            barrier, inc=1, device_id={"tmpl": lax.rem(my_tmpl + step, peers)}, device_id_type=MESH
        )
    for step in range(1, owners):
        pl.semaphore_signal(
            barrier, inc=1, device_id={"sta": lax.rem(my_sta + step, owners)}, device_id_type=MESH
        )
    pl.semaphore_wait(barrier, peers + owners - 2)

    sends = []
    for step in range(1, peers):
        copy = pltpu.make_async_remote_copy(
            src_ref=data_ref,
            dst_ref=gathered.at[my_tmpl],
            send_sem=data_send.at[step],
            recv_sem=data_recv.at[my_tmpl],
            device_id={"tmpl": lax.rem(my_tmpl + step, peers)},
            device_id_type=MESH,
        )
        copy.start()
        sends.append(copy)
    fetches[0].wait()

    for s in range(stations):
        for c in range(channels):
            row = (s * channels + c) * per_group
            flat[row : row + per_group, :] = templates_ref[s, c].astype(jnp.float32)
    waves = flat[...]
    tnorm = jnp.sum(waves * waves, axis=1, keepdims=True)
    norms[...] = jnp.broadcast_to(lax.rsqrt(tnorm / TLEN + EPS) / TLEN, norms.shape)
    down = lax.broadcasted_iota(jnp.int32, (TLEN, TLEN), 0)
    across = lax.broadcasted_iota(jnp.int32, (TLEN, TLEN), 1)
    flip = jnp.where(down + across == TLEN - 1, 1.0, 0.0).astype(jnp.bfloat16)
    flat[...] = jnp.dot(waves.astype(jnp.bfloat16), flip, preferred_element_type=jnp.float32)

    sub = lax.broadcasted_iota(jnp.int32, (8, LANE), 0)
    lane = lax.broadcasted_iota(jnp.int32, (8, LANE), 1)

    def build(group, carry):
        for t in range(per_group):
            row = flat[pl.ds(group * per_group + t, 1), :]
            low = jnp.broadcast_to(row[:, :LANE], (8, LANE))
            high = jnp.broadcast_to(row[:, LANE:], (8, LANE))
            low = pltpu.roll(low, 1, 1, stride=1, stride_axis=0)
            high = pltpu.roll(high, 1, 1, stride=1, stride_axis=0)
            for pair in range(LANE // 16):
                parts = [[], [], []]
                for q in (2 * pair, 2 * pair + 1):
                    keep = lane <= sub + 8 * q
                    first = pltpu.roll(low, 8 * q, 1) if q else low
                    second = pltpu.roll(high, 8 * q, 1) if q else high
                    parts[0].append(jnp.where(keep, second, 0.0))
                    parts[1].append(jnp.where(keep, first, second))
                    parts[2].append(jnp.where(keep, 0.0, first))
                for block in range(3):
                    top = block * LANE + pair * 16
                    bands[group, top : top + 16, t * LANE : (t + 1) * LANE] = jnp.concatenate(
                        parts[block], axis=0
                    ).astype(jnp.bfloat16)
        return carry

    lax.fori_loop(0, groups, build, 0)

    fetches[1].wait()
    fetches[2].wait()
    for step in range(1, peers):
        source = lax.rem(my_tmpl + peers - step, peers)
        pltpu.make_async_remote_copy(
            src_ref=data_ref,
            dst_ref=gathered.at[source],
            send_sem=data_send.at[step],
            recv_sem=data_recv.at[source],
            device_id={"tmpl": source},
            device_id_type=MESH,
        ).wait_recv()
    for c in range(channels):
        whole = jnp.concatenate([gathered[i, c] for i in range(peers)], axis=1)
        for j in range(samples // LANE):
            chunked[pl.ds(c * ROWS + j, stations, stride=channels * ROWS), :] = whole[
                :, j * LANE : (j + 1) * LANE
            ]

    def windows(group):
        return jnp.concatenate(
            [chunked[group * ROWS + i : group * ROWS + i + CHUNKS, :] for i in range(3)], axis=1
        )

    squares = []
    for group in range(groups):
        samples_in = windows(group)
        squares.append(samples_in * samples_in)
    squares = jnp.concatenate(squares, axis=0)
    upper = squares.astype(jnp.bfloat16)
    lower = (squares - upper.astype(jnp.float32)).astype(jnp.bfloat16)
    offset = lax.broadcasted_iota(jnp.int32, (BAND, LANE), 0) - lax.broadcasted_iota(
        jnp.int32, (BAND, LANE), 1
    )
    ones = jnp.where((offset >= 0) & (offset < TLEN), 1.0, 0.0).astype(jnp.bfloat16)
    energy = jnp.dot(upper, ones, preferred_element_type=jnp.float32) + jnp.dot(
        lower, ones, preferred_element_type=jnp.float32
    )
    inverse[...] = lax.rsqrt(energy / TLEN + EPS)

    for group in range(groups):
        raw = jnp.dot(
            windows(group).astype(jnp.bfloat16), bands[group], preferred_element_type=jnp.float32
        )
        local = inverse[group * CHUNKS : (group + 1) * CHUNKS, :]
        for t in range(per_group):
            row = group * per_group + t
            lagged[row, :CHUNKS, :] = raw[:, t * LANE : (t + 1) * LANE] * (
                local * norms[row : row + 1, :]
            )

    zero = jnp.zeros((CHUNKS, LANE), jnp.float32)
    for t in range(per_group):
        same, following = zero, zero
        for s in range(stations):
            for c in range(channels):
                start = starts_ref[c, t, s]
                chunk = start >> 7
                inside = start & (LANE - 1)
                row = (s * channels + c) * per_group + t
                moved = pltpu.roll(lagged[row, pl.ds(chunk, CHUNKS), :], (LANE - inside) & (LANE - 1), 1)
                keep = lane < LANE - inside
                same = same + jnp.where(keep, moved, 0.0)
                following = following + jnp.where(keep, 0.0, moved)
        rows = LAGS // LANE
        partial_ref[:, t, :] = same[:rows] + following[1 : rows + 1]

    span = LAGS // LANE // owners
    for step in range(1, owners):
        target = lax.rem(my_sta + step, owners)
        copy = pltpu.make_async_remote_copy(
            src_ref=partial_ref.at[pl.ds(target * span, span)],
            dst_ref=arrived.at[my_sta],
            send_sem=sum_send.at[step],
            recv_sem=sum_recv.at[my_sta],
            device_id={"sta": target},
            device_id_type=MESH,
        )
        copy.start()
        sends.append(copy)
    total = partial_ref[pl.ds(my_sta * span, span)]
    for step in range(1, owners):
        source = lax.rem(my_sta + owners - step, owners)
        pltpu.make_async_remote_copy(
            src_ref=partial_ref.at[pl.ds(source * span, span)],
            dst_ref=arrived.at[source],
            send_sem=sum_send.at[step],
            recv_sem=sum_recv.at[source],
            device_id={"sta": source},
            device_id_type=MESH,
        ).wait_recv()
        total = total + arrived[source]
    for i in range(span):
        out_ref[:, i * LANE : (i + 1) * LANE] = total[i]
    for copy in sends:
        copy.wait_send()


def shards(data, templates, starts):
    peers, owners = lax.axis_size("tmpl"), lax.axis_size("sta")
    stations, channels, width = data.shape
    per_group = templates.shape[2]
    groups = stations * channels
    vmem = pl.BlockSpec(memory_space=pltpu.VMEM)
    span = LAGS // LANE // owners
    return pl.pallas_call(
        functools.partial(kernel, peers, owners),
        out_shape=jax.ShapeDtypeStruct((per_group, LAGS // owners), jnp.float32),
        in_specs=[pl.BlockSpec(memory_space=pltpu.HBM)] * 3,
        out_specs=vmem,
        scratch_shapes=[
            pltpu.SMEM((channels, per_group, stations), jnp.int32),
            pltpu.VMEM(templates.shape, templates.dtype),
            pltpu.SemaphoreType.DMA((3,)),
            pltpu.VMEM((peers, channels, stations, width), jnp.float32),
            pltpu.VMEM((groups * ROWS, LANE), jnp.float32),
            pltpu.VMEM((groups * per_group, TLEN), jnp.float32),
            pltpu.VMEM((groups, BAND, per_group * LANE), jnp.bfloat16),
            pltpu.VMEM((groups * per_group, LANE), jnp.float32),
            pltpu.VMEM((groups * CHUNKS, LANE), jnp.float32),
            pltpu.VMEM((groups * per_group, ROWS, LANE), jnp.float32),
            pltpu.VMEM((LAGS // LANE, per_group, LANE), jnp.float32),
            pltpu.VMEM((owners, span, per_group, LANE), jnp.float32),
            pltpu.SemaphoreType.DMA((peers,)),
            pltpu.SemaphoreType.DMA((peers,)),
            pltpu.SemaphoreType.DMA((owners,)),
            pltpu.SemaphoreType.DMA((owners,)),
        ],
        compiler_params=pltpu.CompilerParams(
            collective_id=0, has_side_effects=True, vmem_limit_bytes=64 * 1024 * 1024
        ),
    )(jnp.transpose(starts, (1, 2, 0)), jnp.transpose(data, (1, 0, 2)), templates)


def solution(mesh):
    return jax.shard_map(
        shards,
        mesh=mesh,
        in_specs=(
            P(("parts", "sta"), None, "tmpl"),
            P("sta", None, "tmpl", None),
            P("sta", None, "tmpl"),
        ),
        out_specs=P(("parts", "tmpl"), "sta"),
        check_vma=False,
    )
```

```python
import functools

import jax
import jax.numpy as jnp
from jax import lax
from jax.experimental import pallas as pl
from jax.experimental.pallas import tpu as pltpu
from jax.sharding import PartitionSpec as P

TLEN = 256
MAXSHIFT = 512
LAGS = 512
EXTENT = LAGS + MAXSHIFT
LANE = 128
CHUNKS = EXTENT // LANE
BAND = TLEN + LANE
ROWS = 16
EPS = 1e-06

MESH = pl.DeviceIdType.MESH


def kernel(
    peers, owners,
    starts_hbm, data_ref, templates_hbm, out_ref,
    starts_ref, templates_ref, local_sems, gathered, chunked, flat, bands, norms, inverse, lagged, partial_ref, arrived,
    data_send, data_recv, sum_send, sum_recv,
):
    channels, stations, width = data_ref.shape
    per_group = templates_ref.shape[2]
    groups = stations * channels
    samples = width * peers
    my_tmpl = lax.axis_index("tmpl")
    my_sta = lax.axis_index("sta")

    fetches = [
        pltpu.make_async_copy(templates_hbm, templates_ref, local_sems.at[0]),
        pltpu.make_async_copy(starts_hbm, starts_ref, local_sems.at[1]),
        pltpu.make_async_copy(data_ref, gathered.at[my_tmpl], local_sems.at[2]),
    ]
    for copy in fetches:
        copy.start()

    barrier = pltpu.get_barrier_semaphore()
    for step in range(1, peers):
        pl.semaphore_signal(
            barrier, inc=1, device_id={"tmpl": lax.rem(my_tmpl + step, peers)}, device_id_type=MESH
        )
    for step in range(1, owners):
        pl.semaphore_signal(
            barrier, inc=1, device_id={"sta": lax.rem(my_sta + step, owners)}, device_id_type=MESH
        )
    def prepare():
        fetches[0].wait()
        for s in range(stations):
            for c in range(channels):
                row = (s * channels + c) * per_group
                flat[row : row + per_group, :] = templates_ref[s, c].astype(jnp.float32)
        waves = flat[...]
        tnorm = jnp.sum(waves * waves, axis=1, keepdims=True)
        norms[...] = jnp.broadcast_to(lax.rsqrt(tnorm / TLEN + EPS) / TLEN, norms.shape)
        down = lax.broadcasted_iota(jnp.int32, (TLEN, TLEN), 0)
        across = lax.broadcasted_iota(jnp.int32, (TLEN, TLEN), 1)
        flip = jnp.where(down + across == TLEN - 1, 1.0, 0.0).astype(jnp.bfloat16)
        flat[...] = jnp.dot(waves.astype(jnp.bfloat16), flip, preferred_element_type=jnp.float32)

    sub = lax.broadcasted_iota(jnp.int32, (8, LANE), 0)
    lane = lax.broadcasted_iota(jnp.int32, (8, LANE), 1)

    def build(group, carry):
        for t in range(per_group):
            row = flat[pl.ds(group * per_group + t, 1), :]
            low = jnp.broadcast_to(row[:, :LANE], (8, LANE))
            high = jnp.broadcast_to(row[:, LANE:], (8, LANE))
            low = pltpu.roll(low, 1, 1, stride=1, stride_axis=0)
            high = pltpu.roll(high, 1, 1, stride=1, stride_axis=0)
            for pair in range(LANE // 16):
                parts = [[], [], []]
                for q in (2 * pair, 2 * pair + 1):
                    keep = lane <= sub + 8 * q
                    first = pltpu.roll(low, 8 * q, 1) if q else low
                    second = pltpu.roll(high, 8 * q, 1) if q else high
                    parts[0].append(jnp.where(keep, second, 0.0))
                    parts[1].append(jnp.where(keep, first, second))
                    parts[2].append(jnp.where(keep, 0.0, first))
                for block in range(3):
                    top = block * LANE + pair * 16
                    bands[group, top : top + 16, t * LANE : (t + 1) * LANE] = jnp.concatenate(
                        parts[block], axis=0
                    ).astype(jnp.bfloat16)
        return carry

    ahead = my_tmpl * 2 < peers
    early = jnp.where(ahead, groups * 2 // 3 - jnp.minimum(my_tmpl, 1) * (groups // 3), 0)
    pl.when(ahead)(prepare)
    lax.fori_loop(0, early, build, 0)

    pl.semaphore_wait(barrier, peers + owners - 2)

    sends = []
    for step in range(peers - 1):
        target = step + jnp.where(my_tmpl <= step, 1, 0)
        copy = pltpu.make_async_remote_copy(
            src_ref=data_ref,
            dst_ref=gathered.at[my_tmpl],
            send_sem=data_send.at[step],
            recv_sem=data_recv.at[my_tmpl],
            device_id={"tmpl": target},
            device_id_type=MESH,
        )
        copy.start()
        sends.append(copy)

    pl.when(jnp.logical_not(ahead))(prepare)
    lax.fori_loop(early, groups, build, 0)

    fetches[1].wait()
    fetches[2].wait()
    for step in range(1, peers):
        source = lax.rem(my_tmpl + peers - step, peers)
        pltpu.make_async_remote_copy(
            src_ref=data_ref,
            dst_ref=gathered.at[source],
            send_sem=data_send.at[step],
            recv_sem=data_recv.at[source],
            device_id={"tmpl": source},
            device_id_type=MESH,
        ).wait_recv()
    for c in range(channels):
        whole = jnp.concatenate([gathered[i, c] for i in range(peers)], axis=1)
        for j in range(samples // LANE):
            chunked[pl.ds(c * ROWS + j, stations, stride=channels * ROWS), :] = whole[
                :, j * LANE : (j + 1) * LANE
            ]

    def windows(group):
        return jnp.concatenate(
            [chunked[group * ROWS + i : group * ROWS + i + CHUNKS, :] for i in range(3)], axis=1
        )

    squares = []
    for group in range(groups):
        samples_in = windows(group)
        squares.append(samples_in * samples_in)
    squares = jnp.concatenate(squares, axis=0)
    upper = squares.astype(jnp.bfloat16)
    lower = (squares - upper.astype(jnp.float32)).astype(jnp.bfloat16)
    offset = lax.broadcasted_iota(jnp.int32, (BAND, LANE), 0) - lax.broadcasted_iota(
        jnp.int32, (BAND, LANE), 1
    )
    ones = jnp.where((offset >= 0) & (offset < TLEN), 1.0, 0.0).astype(jnp.bfloat16)
    energy = jnp.dot(upper, ones, preferred_element_type=jnp.float32) + jnp.dot(
        lower, ones, preferred_element_type=jnp.float32
    )
    inverse[...] = lax.rsqrt(energy / TLEN + EPS)

    for group in range(groups):
        raw = jnp.dot(
            windows(group).astype(jnp.bfloat16), bands[group], preferred_element_type=jnp.float32
        )
        local = inverse[group * CHUNKS : (group + 1) * CHUNKS, :]
        for t in range(per_group):
            row = group * per_group + t
            lagged[row, :CHUNKS, :] = raw[:, t * LANE : (t + 1) * LANE] * (
                local * norms[row : row + 1, :]
            )

    zero = jnp.zeros((CHUNKS, LANE), jnp.float32)
    for t in range(per_group):
        same, following = zero, zero
        for s in range(stations):
            for c in range(channels):
                start = starts_ref[c, t, s]
                chunk = start >> 7
                inside = start & (LANE - 1)
                row = (s * channels + c) * per_group + t
                moved = pltpu.roll(lagged[row, pl.ds(chunk, CHUNKS), :], (LANE - inside) & (LANE - 1), 1)
                keep = lane < LANE - inside
                same = same + jnp.where(keep, moved, 0.0)
                following = following + jnp.where(keep, 0.0, moved)
        rows = LAGS // LANE
        partial_ref[:, t, :] = same[:rows] + following[1 : rows + 1]

    span = LAGS // LANE // owners
    for step in range(1, owners):
        target = lax.rem(my_sta + step, owners)
        copy = pltpu.make_async_remote_copy(
            src_ref=partial_ref.at[pl.ds(target * span, span)],
            dst_ref=arrived.at[my_sta],
            send_sem=sum_send.at[step],
            recv_sem=sum_recv.at[my_sta],
            device_id={"sta": target},
            device_id_type=MESH,
        )
        copy.start()
        sends.append(copy)
    total = partial_ref[pl.ds(my_sta * span, span)]
    for step in range(1, owners):
        source = lax.rem(my_sta + owners - step, owners)
        pltpu.make_async_remote_copy(
            src_ref=partial_ref.at[pl.ds(source * span, span)],
            dst_ref=arrived.at[source],
            send_sem=sum_send.at[step],
            recv_sem=sum_recv.at[source],
            device_id={"sta": source},
            device_id_type=MESH,
        ).wait_recv()
        total = total + arrived[source]
    for i in range(span):
        out_ref[:, i * LANE : (i + 1) * LANE] = total[i]
    for copy in sends:
        copy.wait_send()


def shards(data, templates, starts):
    peers, owners = lax.axis_size("tmpl"), lax.axis_size("sta")
    stations, channels, width = data.shape
    per_group = templates.shape[2]
    groups = stations * channels
    vmem = pl.BlockSpec(memory_space=pltpu.VMEM)
    span = LAGS // LANE // owners
    return pl.pallas_call(
        functools.partial(kernel, peers, owners),
        out_shape=jax.ShapeDtypeStruct((per_group, LAGS // owners), jnp.float32),
        in_specs=[pl.BlockSpec(memory_space=pltpu.HBM)] * 3,
        out_specs=vmem,
        scratch_shapes=[
            pltpu.SMEM((channels, per_group, stations), jnp.int32),
            pltpu.VMEM(templates.shape, templates.dtype),
            pltpu.SemaphoreType.DMA((3,)),
            pltpu.VMEM((peers, channels, stations, width), jnp.float32),
            pltpu.VMEM((groups * ROWS, LANE), jnp.float32),
            pltpu.VMEM((groups * per_group, TLEN), jnp.float32),
            pltpu.VMEM((groups, BAND, per_group * LANE), jnp.bfloat16),
            pltpu.VMEM((groups * per_group, LANE), jnp.float32),
            pltpu.VMEM((groups * CHUNKS, LANE), jnp.float32),
            pltpu.VMEM((groups * per_group, ROWS, LANE), jnp.float32),
            pltpu.VMEM((LAGS // LANE, per_group, LANE), jnp.float32),
            pltpu.VMEM((owners, span, per_group, LANE), jnp.float32),
            pltpu.SemaphoreType.DMA((peers,)),
            pltpu.SemaphoreType.DMA((peers,)),
            pltpu.SemaphoreType.DMA((owners,)),
            pltpu.SemaphoreType.DMA((owners,)),
        ],
        compiler_params=pltpu.CompilerParams(
            collective_id=0, has_side_effects=True, vmem_limit_bytes=64 * 1024 * 1024
        ),
    )(jnp.transpose(starts, (1, 2, 0)), jnp.transpose(data, (1, 0, 2)), templates)


def solution(mesh):
    return jax.shard_map(
        shards,
        mesh=mesh,
        in_specs=(
            P(("parts", "sta"), None, "tmpl"),
            P("sta", None, "tmpl", None),
            P("sta", None, "tmpl"),
        ),
        out_specs=P(("parts", "tmpl"), "sta"),
        check_vma=False,
    )
```

```python
import functools

import jax
import jax.numpy as jnp
from jax import lax
from jax.experimental import pallas as pl
from jax.experimental.pallas import tpu as pltpu
from jax.sharding import PartitionSpec as P

TLEN = 256
MAXSHIFT = 512
LAGS = 512
EXTENT = LAGS + MAXSHIFT
LANE = 128
CHUNKS = EXTENT // LANE
BAND = TLEN + LANE
ROWS = 16
EPS = 1e-06

MESH = pl.DeviceIdType.MESH


def kernel(
    peers, owners,
    starts_hbm, data_ref, templates_hbm, out_ref,
    starts_ref, templates_ref, local_sems, gathered, chunked, flat, bands, norms, inverse, lagged, partial_ref, arrived,
    data_send, data_recv, sum_send, sum_recv,
):
    channels, stations, width = data_ref.shape
    per_group = templates_ref.shape[2]
    groups = stations * channels
    samples = width * peers
    my_tmpl = lax.axis_index("tmpl")
    my_sta = lax.axis_index("sta")

    fetches = [
        pltpu.make_async_copy(templates_hbm, templates_ref, local_sems.at[0]),
        pltpu.make_async_copy(starts_hbm, starts_ref, local_sems.at[1]),
        pltpu.make_async_copy(data_ref, gathered.at[my_tmpl], local_sems.at[2]),
    ]
    for copy in fetches:
        copy.start()

    barrier = pltpu.get_barrier_semaphore()
    for step in range(1, peers):
        pl.semaphore_signal(
            barrier, inc=1, device_id={"tmpl": lax.rem(my_tmpl + step, peers)}, device_id_type=MESH
        )
    for step in range(1, owners):
        pl.semaphore_signal(
            barrier, inc=1, device_id={"sta": lax.rem(my_sta + step, owners)}, device_id_type=MESH
        )
    def prepare():
        fetches[0].wait()
        for s in range(stations):
            for c in range(channels):
                row = (s * channels + c) * per_group
                flat[row : row + per_group, :] = templates_ref[s, c].astype(jnp.float32)
        waves = flat[...]
        tnorm = jnp.sum(waves * waves, axis=1, keepdims=True)
        norms[...] = jnp.broadcast_to(lax.rsqrt(tnorm / TLEN + EPS) / TLEN, norms.shape)
        down = lax.broadcasted_iota(jnp.int32, (TLEN, TLEN), 0)
        across = lax.broadcasted_iota(jnp.int32, (TLEN, TLEN), 1)
        flip = jnp.where(down + across == TLEN - 1, 1.0, 0.0).astype(jnp.bfloat16)
        flat[...] = jnp.dot(waves.astype(jnp.bfloat16), flip, preferred_element_type=jnp.float32)

    sub = lax.broadcasted_iota(jnp.int32, (8, LANE), 0)
    lane = lax.broadcasted_iota(jnp.int32, (8, LANE), 1)

    def build(group, carry):
        for t in range(per_group):
            row = flat[pl.ds(group * per_group + t, 1), :]
            low = jnp.broadcast_to(row[:, :LANE], (8, LANE))
            high = jnp.broadcast_to(row[:, LANE:], (8, LANE))
            low = pltpu.roll(low, 1, 1, stride=1, stride_axis=0)
            high = pltpu.roll(high, 1, 1, stride=1, stride_axis=0)
            for pair in range(LANE // 16):
                parts = [[], [], []]
                for q in (2 * pair, 2 * pair + 1):
                    keep = lane <= sub + 8 * q
                    first = pltpu.roll(low, 8 * q, 1) if q else low
                    second = pltpu.roll(high, 8 * q, 1) if q else high
                    parts[0].append(jnp.where(keep, second, 0.0))
                    parts[1].append(jnp.where(keep, first, second))
                    parts[2].append(jnp.where(keep, 0.0, first))
                for block in range(3):
                    top = block * LANE + pair * 16
                    bands[group, top : top + 16, t * LANE : (t + 1) * LANE] = jnp.concatenate(
                        parts[block], axis=0
                    ).astype(jnp.bfloat16)
        return carry

    ahead = my_tmpl * 2 < peers
    early = jnp.where(ahead, groups * 2 // 3 - jnp.minimum(my_tmpl, 1) * (groups // 3), 0)
    pl.when(ahead)(prepare)
    lax.fori_loop(0, early, build, 0)

    pl.semaphore_wait(barrier, peers + owners - 2)

    sends = []
    for step in range(peers - 1):
        target = step + jnp.where(my_tmpl <= step, 1, 0)
        copy = pltpu.make_async_remote_copy(
            src_ref=data_ref,
            dst_ref=gathered.at[my_tmpl],
            send_sem=data_send.at[step],
            recv_sem=data_recv.at[my_tmpl],
            device_id={"tmpl": target},
            device_id_type=MESH,
        )
        copy.start()
        sends.append(copy)

    pl.when(jnp.logical_not(ahead))(prepare)
    lax.fori_loop(early, groups, build, 0)

    fetches[1].wait()
    fetches[2].wait()
    for step in range(1, peers):
        source = lax.rem(my_tmpl + peers - step, peers)
        pltpu.make_async_remote_copy(
            src_ref=data_ref,
            dst_ref=gathered.at[source],
            send_sem=data_send.at[step],
            recv_sem=data_recv.at[source],
            device_id={"tmpl": source},
            device_id_type=MESH,
        ).wait_recv()
    for c in range(channels):
        whole = jnp.concatenate([gathered[i, c] for i in range(peers)], axis=1)
        for j in range(samples // LANE):
            chunked[pl.ds(c * ROWS + j, stations, stride=channels * ROWS), :] = whole[
                :, j * LANE : (j + 1) * LANE
            ]

    def windows(group):
        return jnp.concatenate(
            [chunked[group * ROWS + i : group * ROWS + i + CHUNKS, :] for i in range(3)], axis=1
        )

    squares = []
    for group in range(groups):
        samples_in = windows(group)
        squares.append(samples_in * samples_in)
    squares = jnp.concatenate(squares, axis=0)
    upper = squares.astype(jnp.bfloat16)
    lower = (squares - upper.astype(jnp.float32)).astype(jnp.bfloat16)
    offset = lax.broadcasted_iota(jnp.int32, (BAND, LANE), 0) - lax.broadcasted_iota(
        jnp.int32, (BAND, LANE), 1
    )
    ones = jnp.where((offset >= 0) & (offset < TLEN), 1.0, 0.0).astype(jnp.bfloat16)
    energy = jnp.dot(upper, ones, preferred_element_type=jnp.float32) + jnp.dot(
        lower, ones, preferred_element_type=jnp.float32
    )
    inverse[...] = lax.rsqrt(energy / TLEN + EPS)

    for group in range(groups):
        raw = jnp.dot(
            windows(group).astype(jnp.bfloat16), bands[group], preferred_element_type=jnp.float32
        )
        local = inverse[group * CHUNKS : (group + 1) * CHUNKS, :]
        for t in range(per_group):
            row = group * per_group + t
            lagged[row, :CHUNKS, :] = raw[:, t * LANE : (t + 1) * LANE] * (
                local * norms[row : row + 1, :]
            )

    zero = jnp.zeros((CHUNKS, LANE), jnp.float32)
    for t in range(per_group):
        same, following = zero, zero
        for s in range(stations):
            for c in range(channels):
                start = starts_ref[c, t, s]
                chunk = start >> 7
                inside = start & (LANE - 1)
                row = (s * channels + c) * per_group + t
                moved = pltpu.roll(lagged[row, pl.ds(chunk, CHUNKS), :], (LANE - inside) & (LANE - 1), 1)
                keep = lane < LANE - inside
                same = same + jnp.where(keep, moved, 0.0)
                following = following + jnp.where(keep, 0.0, moved)
        rows = LAGS // LANE
        partial_ref[:, t, :] = same[:rows] + following[1 : rows + 1]

    span = LAGS // LANE // owners
    for step in range(owners - 1):
        target = step + jnp.where(my_sta <= step, 1, 0)
        copy = pltpu.make_async_remote_copy(
            src_ref=partial_ref.at[pl.ds(target * span, span)],
            dst_ref=arrived.at[my_sta],
            send_sem=sum_send.at[step],
            recv_sem=sum_recv.at[my_sta],
            device_id={"sta": target},
            device_id_type=MESH,
        )
        copy.start()
        sends.append(copy)
    total = partial_ref[pl.ds(my_sta * span, span)]
    for step in range(1, owners):
        source = lax.rem(my_sta + owners - step, owners)
        pltpu.make_async_remote_copy(
            src_ref=partial_ref.at[pl.ds(source * span, span)],
            dst_ref=arrived.at[source],
            send_sem=sum_send.at[step],
            recv_sem=sum_recv.at[source],
            device_id={"sta": source},
            device_id_type=MESH,
        ).wait_recv()
        total = total + arrived[source]
    for i in range(span):
        out_ref[:, i * LANE : (i + 1) * LANE] = total[i]
    for copy in sends:
        copy.wait_send()


def shards(data, templates, starts):
    peers, owners = lax.axis_size("tmpl"), lax.axis_size("sta")
    stations, channels, width = data.shape
    per_group = templates.shape[2]
    groups = stations * channels
    vmem = pl.BlockSpec(memory_space=pltpu.VMEM)
    span = LAGS // LANE // owners
    return pl.pallas_call(
        functools.partial(kernel, peers, owners),
        out_shape=jax.ShapeDtypeStruct((per_group, LAGS // owners), jnp.float32),
        in_specs=[pl.BlockSpec(memory_space=pltpu.HBM)] * 3,
        out_specs=vmem,
        scratch_shapes=[
            pltpu.SMEM((channels, per_group, stations), jnp.int32),
            pltpu.VMEM(templates.shape, templates.dtype),
            pltpu.SemaphoreType.DMA((3,)),
            pltpu.VMEM((peers, channels, stations, width), jnp.float32),
            pltpu.VMEM((groups * ROWS, LANE), jnp.float32),
            pltpu.VMEM((groups * per_group, TLEN), jnp.float32),
            pltpu.VMEM((groups, BAND, per_group * LANE), jnp.bfloat16),
            pltpu.VMEM((groups * per_group, LANE), jnp.float32),
            pltpu.VMEM((groups * CHUNKS, LANE), jnp.float32),
            pltpu.VMEM((groups * per_group, ROWS, LANE), jnp.float32),
            pltpu.VMEM((LAGS // LANE, per_group, LANE), jnp.float32),
            pltpu.VMEM((owners, span, per_group, LANE), jnp.float32),
            pltpu.SemaphoreType.DMA((peers,)),
            pltpu.SemaphoreType.DMA((peers,)),
            pltpu.SemaphoreType.DMA((owners,)),
            pltpu.SemaphoreType.DMA((owners,)),
        ],
        compiler_params=pltpu.CompilerParams(
            collective_id=0, has_side_effects=True, vmem_limit_bytes=64 * 1024 * 1024 - 10559488
        ),
    )(jnp.transpose(starts, (1, 2, 0)), jnp.transpose(data, (1, 0, 2)), templates)


def solution(mesh):
    return jax.shard_map(
        shards,
        mesh=mesh,
        in_specs=(
            P(("parts", "sta"), None, "tmpl"),
            P("sta", None, "tmpl", None),
            P("sta", None, "tmpl"),
        ),
        out_specs=P(("parts", "tmpl"), "sta"),
        check_vma=False,
    )
```
